32 devices in a mesh: dp: 8 (over z, y), tensor: 4 (over x, core).
Axes of the slice: x: 2, y: 2, z: 4, core: 2. Of those that a mesh axis runs over, the one named last changes fastest.
Arguments:
- tokens: bfloat16 [24, 736, 768], P('dp', None, 'tensor'), may hold values from -6 to 6
- horizon: int32 [24], P('dp'), may hold values from 4 to 30, as said below
- attn_gain: float32 [768], replicated, may hold values from 0.5 to 1.5
- attn_shift: float32 [768], replicated, may hold values from -1.5 to 1.5
- query_weight: bfloat16 [768, 768], P(None, 'tensor'), may hold values from -0.21875 to 0.21875
- key_weight: bfloat16 [768, 768], P(None, 'tensor'), may hold values from -0.21875 to 0.21875
- value_weight: bfloat16 [768, 768], P(None, 'tensor'), may hold values from -0.21875 to 0.21875
- query_bias: float32 [768], P('tensor'), may hold values from -2.5 to 2.5
- value_bias: float32 [768], P('tensor'), may hold values from -2.5 to 2.5
- output_weight: bfloat16 [768, 768], P('tensor'), may hold values from -0.625 to 0.625
- output_bias: float32 [768], P('tensor'), may hold values from -1.5 to 1.5
- mlp_gain: float32 [768], replicated, may hold values from 0.5 to 1.5
- mlp_shift: float32 [768], replicated, may hold values from -1.5 to 1.5
- up_weight: bfloat16 [768, 3072], P(None, 'tensor'), may hold values from -0.21875 to 0.21875
- up_bias: float32 [3072], P('tensor'), may hold values from -2.5 to 2.5
- down_weight: bfloat16 [3072, 768], P('tensor'), may hold values from -0.15625 to 0.15625
- down_bias: float32 [768], P('tensor'), may hold values from -1.5 to 1.5
- cotangent: bfloat16 [24, 736, 768], P('dp', None, 'tensor'), may hold values from -6 to 6
Outputs:
- result: bfloat16 [24, 736, 768], P('dp', None, 'tensor')
- grad_tokens: bfloat16 [24, 736, 768], P('dp', None, 'tensor')
- grad_attn_gain: float32 [768], P('tensor')
- grad_attn_shift: float32 [768], P('tensor')
- grad_query_weight: float32 [768, 768], P(None, 'tensor')
- grad_key_weight: float32 [768, 768], P(None, 'tensor')
- grad_value_weight: float32 [768, 768], P(None, 'tensor')
- grad_query_bias: float32 [768], P('tensor')
- grad_value_bias: float32 [768], P('tensor')
- grad_output_weight: float32 [768, 768], P('tensor')
- grad_output_bias: float32 [768], P('tensor')
- grad_mlp_gain: float32 [768], P('tensor')
- grad_mlp_shift: float32 [768], P('tensor')
- grad_up_weight: float32 [768, 3072], P(None, 'tensor')
- grad_up_bias: float32 [3072], P('tensor')
- grad_down_weight: float32 [3072, 768], P('tensor')
- grad_down_bias: float32 [768], P('tensor')
The draws below stay inside these ranges and needn't reach their ends.
Inputs may be any that keep to these rules, and one draw needn't show every extreme that they name: horizon[c] is the number of future frames of clip c; the clip's first 256 + 16 * horizon[c] rows are real, the rest of its 736 rows are padding.
All inputs are finite; a program needn't handle non-finite values.
Results may differ from the reference program's by a relative error of at most 0.012.
Values may be sent and summed in bfloat16 or wider, within the bound.
No kernel may reach another device: no remote copies, remote signals or barrier semaphores. Data moves between devices by JAX's collectives and lax.ppermute only.
A program may use at most 192 MiB of HBM per device.

```python
import jax
import jax.numpy as jnp
from jax import lax

D = 768
HEADS = 12
HDIM = 64
FF = 3072
CONTEXT = 256
FRAME = 16
HMIN = 4
HMAX = 30
CLIP = 736
CLIPS = 24


def draw_horizon(key, part):
    first_key, second_key, spot_key, other_key = jax.random.split(key, 4)
    first = jax.random.randint(first_key, (CLIPS,), HMIN, HMAX + 1, dtype=jnp.int32)
    second = jax.random.randint(second_key, (CLIPS,), HMIN, HMAX + 1, dtype=jnp.int32)
    frames = jnp.maximum(first, second)
    spot = jax.random.randint(spot_key, (), 0, CLIPS, dtype=jnp.int32)
    other = (spot + 1 + jax.random.randint(other_key, (), 0, CLIPS - 1, dtype=jnp.int32)) % CLIPS
    frames = frames.at[spot].set(HMAX)
    frames = frames.at[other].set(HMIN)
    return frames.astype(jnp.int32)


def block_levels(own_key, dims, cuts, least, high):
    loudness, own = 1.0, jax.random.fold_in(own_key, 6)
    for dim, parts in cuts:
        heights = jnp.exp(jax.random.uniform(jax.random.fold_in(own, dim), (parts,), jnp.float32, least / len(cuts), high / len(cuts)))
        loudness = loudness * jnp.repeat(heights, dims[dim] // parts).reshape([-1 if axis == dim else 1 for axis in range(len(dims))])
    return loudness


def scatter_about(stream_key, extent, width, reach, cuts=(), kind=jnp.bfloat16):
    factor_of = block_levels(stream_key, extent, cuts, -0.22, 0.18) if cuts else 1.0
    values = jax.random.normal(stream_key, extent, jnp.float32) * width * factor_of
    return jnp.minimum(jnp.maximum(values, -reach), reach).astype(kind)


def setup_inputs(seed: int = 0) -> dict:
    keys = jax.random.split(jax.random.key(seed), 19)
    return {
        "tokens": scatter_about(keys[0], (CLIPS, CLIP, D), 1.0, 6.0, ((0, 8), (2, 4))),
        "horizon": draw_horizon(jax.random.fold_in(keys[18], 71), 0),
        "attn_gain": jnp.clip(1.0 + 0.1 * jax.random.normal(keys[2], (D,), jnp.float32), 0.5, 1.5),
        "attn_shift": scatter_about(keys[3], (D,), 0.3, 1.5, (), jnp.float32),
        "query_weight": scatter_about(keys[4], (D, HEADS * HDIM), D ** -0.5, 0.21875, ((1, 4),)),
        "key_weight": scatter_about(keys[5], (D, HEADS * HDIM), D ** -0.5, 0.21875, ((1, 4),)),
        "value_weight": scatter_about(keys[6], (D, HEADS * HDIM), D ** -0.5, 0.21875, ((1, 4),)),
        "query_bias": scatter_about(keys[7], (HEADS * HDIM,), 0.5, 2.5, ((0, 4),), jnp.float32),
        "value_bias": scatter_about(keys[8], (HEADS * HDIM,), 0.5, 2.5, ((0, 4),), jnp.float32),
        "output_weight": scatter_about(keys[9], (HEADS * HDIM, D), (D // 8) ** -0.5, 0.625, ((0, 4),)),
        "output_bias": scatter_about(keys[10], (D,), 0.3, 1.5, ((0, 4),), jnp.float32),
        "mlp_gain": jnp.clip(1.0 + 0.1 * jax.random.normal(keys[11], (D,), jnp.float32), 0.5, 1.5),
        "mlp_shift": scatter_about(keys[12], (D,), 0.3, 1.5, (), jnp.float32),
        "up_weight": scatter_about(keys[13], (D, FF), D ** -0.5, 0.21875, ((1, 4),)),
        "up_bias": scatter_about(keys[14], (FF,), 0.5, 2.5, ((0, 4),), jnp.float32),
        "down_weight": scatter_about(keys[15], (FF, D), (FF // 2) ** -0.5, 0.15625, ((0, 4),)),
        "down_bias": scatter_about(keys[16], (D,), 0.3, 1.5, ((0, 4),), jnp.float32),
        "cotangent": scatter_about(keys[17], (CLIPS, CLIP, D), 1.0, 6.0, ((0, 8), (2, 4))),
    }


EPS = 1e-05
NEGATIVE = -1e+30

@jax.custom_vjp
def low(v):
    return lax.optimization_barrier(v.astype(jnp.bfloat16)).astype(jnp.float32)

@jax.custom_vjp
def low_back(v):
    return v

def low_keep(v):
    return (low(v), None)

def low_pass(kept, grad):
    return (grad,)

def back_keep(v):
    return (v, None)

def back_low(kept, grad):
    return (low(grad),)
low.defvjp(low_keep, low_pass)
low_back.defvjp(back_keep, back_low)

def matmul(left, right):
    return jnp.dot(left, right, precision=lax.Precision.HIGHEST)

def layer_norm(rows, gain, shift):
    row_mean = lax.optimization_barrier(jnp.mean(rows, axis=-1, keepdims=True))
    centered = rows - row_mean
    row_var = lax.optimization_barrier(jnp.mean(centered * centered, axis=-1, keepdims=True))
    return centered * lax.rsqrt(row_var + EPS) * gain + shift

def clip_forward(params, tokens_clip, length):
    attn_gain, attn_shift, query_weight, key_weight, value_weight, query_bias, value_bias, output_weight, output_bias, mlp_gain, mlp_shift, up_weight, up_bias, down_weight, down_bias = params
    normed = low(layer_norm(tokens_clip, attn_gain, attn_shift))
    queries = low(low_back(matmul(normed, query_weight) + query_bias))
    keys_all = low(low_back(matmul(normed, key_weight)))
    values = low(low_back(matmul(normed, value_weight) + value_bias))
    shaped = (CLIP, HEADS, HDIM)
    scores = jnp.einsum('qhd,khd->hqk', queries.reshape(shaped), keys_all.reshape(shaped), precision=lax.Precision.HIGHEST)
    scores = low_back(scores * HDIM ** (-0.5))
    position = jnp.arange(CLIP, dtype=jnp.int32)
    allowed = (position[None, :] <= position[:, None]) & (position[None, :] < length)
    scores = jnp.where(allowed[None], scores, NEGATIVE)
    attn_prob = low(jax.nn.softmax(scores, axis=-1))
    mixed = jnp.einsum('hqk,khd->qhd', attn_prob, values.reshape(shaped), precision=lax.Precision.HIGHEST).reshape(CLIP, HEADS * HDIM)
    mixed = low(low_back(mixed))
    middle = tokens_clip + low_back(matmul(mixed, output_weight)) + output_bias
    normed_two = low(layer_norm(low(middle), mlp_gain, mlp_shift))
    hidden_pre = low_back(matmul(normed_two, up_weight) + up_bias)
    hidden = low(jax.nn.gelu(hidden_pre, approximate=True))
    return middle + low_back(matmul(hidden, down_weight)) + down_bias

def reference(tokens, horizon, attn_gain, attn_shift, query_weight, key_weight, value_weight, query_bias, value_bias, output_weight, output_bias, mlp_gain, mlp_shift, up_weight, up_bias, down_weight, down_bias, cotangent):
    params = tuple((param.astype(jnp.float32) for param in (attn_gain, attn_shift, query_weight, key_weight, value_weight, query_bias, value_bias, output_weight, output_bias, mlp_gain, mlp_shift, up_weight, up_bias, down_weight, down_bias)))
    lengths = (CONTEXT + FRAME * horizon).astype(jnp.int32)
    stepper = jax.checkpoint(clip_forward)

    def run(weights, rows):
        return lax.map(lambda pieces: stepper(weights, pieces[0], pieces[1]), (rows, lengths))
    result, pullback = jax.vjp(run, params, tokens.astype(jnp.float32))
    valid = (jnp.arange(CLIP, dtype=jnp.int32)[None, :] < lengths[:, None]).astype(jnp.float32)
    grads, grad_rows = pullback(cotangent.astype(jnp.float32) * valid[:, :, None])
    return (result.astype(jnp.bfloat16), grad_rows.astype(jnp.bfloat16), grads[0], grads[1], grads[2], grads[3], grads[4], grads[5], grads[6], grads[7], grads[8], grads[9], grads[10], grads[11], grads[12], grads[13], grads[14])
```

```python
from functools import partial

import jax
import jax.numpy as jnp
from jax import lax
from jax.experimental import pallas as pl
from jax.experimental.pallas import tpu as pltpu
from jax.sharding import PartitionSpec as P

HDIM = 64
CONTEXT = 256
FRAME = 16
EPS = 1e-05
NEGATIVE = -1e30
LOG2E = 1.4426950408889634

F32 = jnp.float32
BF16 = jnp.bfloat16
QB = 256
LB = 128
TAIL = 16


VM = pl.BlockSpec(memory_space=pltpu.VMEM)
SM = pl.BlockSpec(memory_space=pltpu.SMEM)


def call(body, name, outs, args, scratch=(), flops=0, trans=0, specs=None):
    size = sum(a.size * a.dtype.itemsize for a in args)
    size += sum(o.size * o.dtype.itemsize for o in outs)
    in_specs = [SM] + [VM] * (len(args) - 1)
    for place, spec in (specs or {}).items():
        in_specs[place] = spec
    return pl.pallas_call(
        body,
        out_shape=tuple(outs),
        grid=(1,) if specs else (),
        in_specs=in_specs,
        out_specs=tuple([VM] * len(outs)),
        scratch_shapes=list(scratch),
        compiler_params=pltpu.CompilerParams(vmem_limit_bytes=56 * 1024 * 1024),
        cost_estimate=pl.CostEstimate(
            flops=int(flops), bytes_accessed=int(size), transcendentals=int(trans)
        ),
        name=name,
    )(*args)


def struct(shape, dtype):
    return jax.ShapeDtypeStruct(shape, dtype)


def dot(left, right):
    return jnp.dot(left, right, preferred_element_type=F32)


def dot_nt(left, right):
    return lax.dot_general(left, right, (((1,), (1,)), ((), ())), preferred_element_type=F32)


def iota(shape, dim):
    return lax.broadcasted_iota(jnp.int32, shape, dim)


def lanes_loop(count, body):
    def one(i, carry):
        body(pl.ds(pl.multiple_of(i * LB, LB), LB), i * LB)
        return carry

    lax.fori_loop(0, count // LB, one, 0)


def wide(column, count):
    return jnp.concatenate([column] * (count // LB), axis=1)


def shard_rows(t, j, width):
    return pl.ds(pl.multiple_of((t ^ j) * width, width), width)


def row_sums(x):
    part = x[:, :LB]
    for n in range(1, x.shape[1] // LB):
        part = part + x[:, n * LB : (n + 1) * LB]
    ones = jnp.ones((8, LB), F32)
    return lax.dot_general(
        ones, part, (((1,), (1,)), ((), ())),
        preferred_element_type=F32, precision=lax.Precision.HIGHEST,
    )[0:1]


def transposed(x):
    return jnp.transpose(x.astype(F32)).astype(BF16)


def prep_kernel(info, w, up, down, w_o, up_o, down_o):
    w_o[...] = transposed(w[...])
    up_o[...] = transposed(up[...])
    down_o[...] = transposed(down[...])


def prep_out_kernel(info, w0, w1, w2, w3, wt_o, bias_o):
    t = info[0]
    full = w0.shape[1]
    width = full // 4
    for j, w in enumerate((w0, w1, w2, w3)):
        wt_o[:, j * width : (j + 1) * width] = transposed(w[0:width, :])
        tail = w[width : width + TAIL, :].astype(F32)
        bias = jnp.broadcast_to((tail[0:1] + tail[1:2])[:, : 2 * LB], (LB, 2 * LB))
        bias_o[shard_rows(t, j, width), :] = jnp.transpose(bias)[0:width, :]


def attention_masks(j, length):
    key = iota((QB, QB), 0)
    query = iota((QB, QB), 1)
    causal = key <= query
    short = None
    if (j + 1) * QB > CONTEXT:
        short = key < length - j * QB
        causal = causal & short
    return causal, short


def norm_stats(x, full):
    mean = jnp.sum(x, axis=0, keepdims=True) * (1.0 / full)
    centered = x - mean
    var = jnp.sum(centered * centered, axis=0, keepdims=True) * (1.0 / full)
    inv = lax.rsqrt(var + EPS)
    return mean, inv, centered * inv


def fwd_kernel(
    clip, info, t0, t1, t2, t3, gain, shift, w, b,
    tok_o, acts_o, qkv_o, ob_o, of_o, lse_o, stat_o,
):
    width, rows_all = t0.shape
    full, padded = tok_o.shape
    t = info[0]
    length = info[1 + clip]
    for j, src in enumerate((t0, t1, t2, t3)):
        dst = shard_rows(t, j, width)
        tok_o[dst, 0:rows_all] = src[...]
        tok_o[dst, rows_all:] = jnp.zeros((width, padded - rows_all), BF16)
    stat_o[...] = jnp.zeros_like(stat_o)
    lse_o[...] = jnp.zeros_like(lse_o)

    def norm(cols, first):
        mean, inv, normed = norm_stats(tok_o[:, cols].astype(F32), full)
        acts_o[:, cols] = (normed * gain[...] + shift[...]).astype(BF16)
        stat_o[0:1, cols] = mean
        stat_o[1:2, cols] = inv

    lanes_loop(padded, norm)
    qkv = dot(w[...], acts_o[...]) + wide(b[...], padded)
    qkv_o[...] = qkv.astype(BF16)
    factor = LOG2E * HDIM ** (-0.5)
    for h in range(width // HDIM):
        part = slice(h * HDIM, (h + 1) * HDIM)
        qt = qkv_o[part, :]
        kn = transposed(qkv_o[width + h * HDIM : width + (h + 1) * HDIM, :])
        vt = qkv_o[2 * width + h * HDIM : 2 * width + (h + 1) * HDIM, :]
        for i in range(padded // QB):
            block = slice(i * QB, (i + 1) * QB)
            scores = []
            top = None
            for j in range(i + 1):
                s = dot(kn[j * QB : (j + 1) * QB, :], qt[:, block])
                causal, short = attention_masks(j, length)
                if i == j:
                    s = jnp.where(causal, s, NEGATIVE)
                elif short is not None:
                    s = jnp.where(short, s, NEGATIVE)
                scores.append(s)
                high = jnp.max(s, axis=0, keepdims=True)
                top = high if top is None else jnp.maximum(top, high)
            base = top * factor
            total = jnp.zeros((1, QB), F32)
            acc = jnp.zeros((HDIM, QB), F32)
            for j in range(i + 1):
                e = jnp.exp2(scores[j] * factor - base)
                total = total + jnp.sum(e, axis=0, keepdims=True)
                acc = acc + dot(vt[:, j * QB : (j + 1) * QB], e.astype(BF16))
            out = acc / total
            of_o[part, block] = out
            ob_o[part, block] = out.astype(BF16)
            lse_o[h : h + 1, block] = base + jnp.log2(total)


def mean_rows(m1, m2, place):
    row = iota((TAIL, m1.shape[1]), 0)
    h1 = m1.astype(BF16).astype(F32)
    h2 = m2.astype(BF16).astype(F32)
    out = jnp.zeros((TAIL, m1.shape[1]), F32)
    for n, value in enumerate((h1, m1 - h1, h2, m2 - h2)):
        out = jnp.where(row == place + n, value, out)
    return out


def pack_parts(t, acc, stat, width, p0, p13, p2):
    m1, m2 = stat[2:3, :], stat[3:4, :]
    p0[0:width, :] = acc[shard_rows(t, 0, width), :]
    p0[width : width + TAIL, :] = mean_rows(m1, m2, 0)
    low = mean_rows(m1, m2, 4).astype(BF16)
    for n, j in enumerate((1, 3)):
        p13[n, 0:width, :] = acc[shard_rows(t, j, width), :].astype(BF16)
        p13[n, width : width + TAIL, :] = low
    p2[0:width, :] = acc[shard_rows(t, 2, width), :].astype(BF16)
    p2[width : width + TAIL, :] = mean_rows(m1, m2, 0).astype(BF16)


def mlp_kernel(
    clip, info, tok, o0, o1, o2, o3, wot, ob, gain, shift, up, upt, down, downt, ub, db,
    c0, c1, c2, c3,
    hid_o, dpre_o, acts_o, dy_o, ubsum_o, r0_o, r2_o, s13_o, p0_o, p2_o, norm_o, stat_o,
    mid_s, acc_s, ox_s,
):
    full, padded = tok.shape
    width, rows_all = c0.shape
    t = info[0]
    length = info[1 + clip]
    for j, src in enumerate((o0, o1, o2, o3)):
        ox_s[j * width : (j + 1) * width, :] = src[...]
    mid_s[...] = dot(wot[...], ox_s[...])
    for j, src in enumerate((c0, c1, c2, c3)):
        dst = shard_rows(t, j, width)
        live = iota((width, rows_all), 1) < length
        dy_o[dst, 0:rows_all] = jnp.where(live, src[...].astype(F32), 0.0).astype(BF16)
        dy_o[dst, rows_all:] = jnp.zeros((width, padded - rows_all), BF16)
    stat_o[...] = jnp.zeros_like(stat_o)

    def norm(cols, first):
        mid = mid_s[:, cols] + tok[:, cols].astype(F32) + ob[...]
        mid_s[:, cols] = mid
        mean, inv, normed = norm_stats(mid.astype(BF16).astype(F32), full)
        acts_o[:, cols] = (normed * gain[...] + shift[...]).astype(BF16)
        stat_o[0:1, cols] = mean
        stat_o[1:2, cols] = inv

    lanes_loop(padded, norm)
    c_in = 0.7978845608028654
    c_cu = c_in * 0.044715
    ubsum_o[...] = jnp.zeros_like(ubsum_o)
    tile = 256
    for n in range(full // tile):
        part = slice(n * tile, (n + 1) * tile)
        u = dot(upt[part, :], acts_o[...]) + wide(ub[part, :], padded)
        dh = dot(down[part, :], dy_o[...])
        u2 = u * u
        th = jnp.tanh(u * (c_in + c_cu * u2))
        half = 0.5 + 0.5 * th
        hid_o[part, :] = (u * half).astype(BF16)
        slope = half + u * (1.0 - th * th) * (0.5 * c_in + 1.5 * c_cu * u2)
        dpre = dh * slope
        dpre_o[part, :] = dpre.astype(BF16)
        ubsum_o[0:1, part] = row_sums(dpre)

    acc_s[...] = dot(up[...], dpre_o[...])

    def stats(cols, first):
        normed = (mid_s[:, cols].astype(BF16).astype(F32) - stat_o[0:1, cols]) * stat_o[1:2, cols]
        scaled = acc_s[:, cols] * gain[...]
        stat_o[2:3, cols] = jnp.sum(scaled, axis=0, keepdims=True) * (1.0 / full)
        stat_o[3:4, cols] = jnp.sum(scaled * normed, axis=0, keepdims=True) * (1.0 / full)

    lanes_loop(padded, stats)
    pack_parts(t, acc_s, stat_o, width, p0_o, s13_o, p2_o)
    own = mid_s[shard_rows(t, 0, width), :]
    norm_o[...] = (own.astype(BF16).astype(F32) - stat_o[0:1, :]) * stat_o[1:2, :]

    acc_s[...] = dot(downt[...], hid_o[...])
    r0_o[...] = acc_s[shard_rows(t, 0, width), :] + own + wide(db[...], padded)
    for n, j in enumerate((1, 3)):
        s13_o[n, width + TAIL :, :] = acc_s[shard_rows(t, j, width), :].astype(BF16)
    r2_o[...] = acc_s[shard_rows(t, 2, width), :].astype(BF16)


def summed_part(p0, got, far, width):
    x = p0[...] + got[0].astype(F32) + far[...].astype(F32)
    ext = x[width:, :]
    m1 = ext[0:1] + ext[1:2] + ext[4:5] + ext[5:6]
    m2 = ext[2:3] + ext[3:4] + ext[6:7] + ext[7:8]
    return x[0:width, :], m1, m2


def mid_kernel(clip, info, p0, got, far, normed, stat, cot, gain, dmid_o, dmidb_o, sums_o):
    width, rows_all = cot.shape
    padded = p0.shape[1]
    length = info[1 + clip]
    g, m1, m2 = summed_part(p0, got, far, width)
    live = iota((width, rows_all), 1) < length
    dy = jnp.where(live, cot[...].astype(F32), 0.0)
    dy = jnp.concatenate([dy, jnp.zeros((width, padded - rows_all), F32)], axis=1)
    normed = normed[...]
    dmid = dy + stat[1:2, :] * (g * wide(gain[...], padded) - m1 - normed * m2)
    dmid_o[...] = dmid
    dmidb_o[...] = dmid.astype(BF16)
    sums_o[...] = jnp.zeros_like(sums_o)
    sums_o[0:1, :] = row_sums(dmid)
    sums_o[1:2, :] = row_sums(g * normed)
    sums_o[2:3, :] = row_sums(g)
    sums_o[3:4, :] = row_sums(dy)


def bwd_kernel(
    clip, info, d0, d1, d2, d3, wo, qkv, of, ob, lse, tok, acts, stat, gain, w, *refs
):
    prior = refs[0] if clip else None
    refs = refs[1:] if clip else refs
    acc_o, sums_o, p0_o, p13_o, p2_o, d_s, do_s, dqkv_s, acc_s, stat_s = refs
    full, padded = tok.shape
    width = of.shape[0]
    t = info[0]
    length = info[1 + clip]
    for j, src in enumerate((d0, d1, d2, d3)):
        d_s[shard_rows(t, j, width), :] = src[...]
    do_s[...] = dot(wo[...], d_s[...]).astype(BF16)
    factor = LOG2E * HDIM ** (-0.5)
    scale = HDIM ** (-0.5)
    blocks = padded // QB
    for h in range(width // HDIM):
        part = slice(h * HDIM, (h + 1) * HDIM)
        kpart = slice(width + h * HDIM, width + (h + 1) * HDIM)
        vpart = slice(2 * width + h * HDIM, 2 * width + (h + 1) * HDIM)
        qt, kt, dot_ = qkv[part, :], qkv[kpart, :], do_s[part, :]
        qn, kn, vn, don = (transposed(x) for x in (qt, kt, qkv[vpart, :], dot_))
        delta = jnp.sum(of[part, :] * dot_.astype(F32), axis=0, keepdims=True)
        base = lse[h : h + 1, :]
        dq = [jnp.zeros((HDIM, QB), F32) for _ in range(blocks)]
        dk, dv = [], []
        for j in range(blocks):
            block = slice(j * QB, (j + 1) * QB)
            causal, short = attention_masks(j, length)
            dk_j = jnp.zeros((QB, HDIM), F32)
            dv_j = jnp.zeros((QB, HDIM), F32)
            for i in range(j, blocks):
                late = slice(i * QB, (i + 1) * QB)
                s = dot(kn[block, :], qt[:, late])
                p = jnp.exp2(s * factor - base[:, late])
                if i == j:
                    p = jnp.where(causal, p, 0.0)
                elif short is not None:
                    p = jnp.where(short, p, 0.0)
                dp = dot(vn[block, :], dot_[:, late])
                ds = (p * (dp - delta[:, late])).astype(BF16)
                dv_j = dv_j + dot(p.astype(BF16), don[late, :])
                dk_j = dk_j + dot(ds, qn[late, :])
                dq[i] = dq[i] + dot(kt[:, block], ds)
            dk.append(dk_j)
            dv.append(dv_j)
        dqkv_s[part, :] = (jnp.concatenate(dq, axis=1) * scale).astype(BF16)
        dqkv_s[kpart, :] = (jnp.transpose(jnp.concatenate(dk, axis=0)) * scale).astype(BF16)
        dqkv_s[vpart, :] = jnp.transpose(jnp.concatenate(dv, axis=0)).astype(BF16)

    acc_s[...] = dot(w[...], dqkv_s[...])

    def stats(cols, first):
        normed = (tok[:, cols].astype(F32) - stat[0:1, cols]) * stat[1:2, cols]
        scaled = acc_s[:, cols] * gain[...]
        stat_s[2:3, cols] = jnp.sum(scaled, axis=0, keepdims=True) * (1.0 / full)
        stat_s[3:4, cols] = jnp.sum(scaled * normed, axis=0, keepdims=True) * (1.0 / full)

    lanes_loop(padded, stats)
    pack_parts(t, acc_s, stat_s, width, p0_o, p13_o, p2_o)
    sums_o[...] = jnp.zeros_like(sums_o)
    sums_o[0:1, :] = row_sums(dqkv_s[0:width, :].astype(F32))
    sums_o[1:2, :] = row_sums(dqkv_s[2 * width :, :].astype(F32))
    top = dot_nt(dqkv_s[...], acts[...])
    low = dot_nt(ob[...], d_s[...])
    if clip:
        top = top + prior[0 : 3 * width, :]
        low = low + prior[3 * width :, :]
    acc_o[0 : 3 * width, :] = top
    acc_o[3 * width :, :] = low


def final_kernel(info, p0, got, far, own, stat, dmid, gain, out_o, sums_o):
    width, rows_all = own.shape
    padded = p0.shape[1]
    g, m1, m2 = summed_part(p0, got, far, width)
    x = own[...].astype(F32)
    x = jnp.concatenate([x, jnp.zeros((width, padded - rows_all), F32)], axis=1)
    normed = (x - stat[0:1, :]) * stat[1:2, :]
    grad = dmid[...] + stat[1:2, :] * (g * wide(gain[...], padded) - m1 - normed * m2)
    out_o[...] = grad[:, 0:rows_all].astype(BF16)
    sums_o[...] = jnp.zeros_like(sums_o)
    sums_o[0:1, :] = row_sums(g * normed)
    sums_o[1:2, :] = row_sums(g)


def slot_of(index, group, bits):
    p = index ^ group
    place = (p & 1) << (bits - 1)
    for b in range(1, bits):
        place = place | (((p >> b) & 1) << (bits - 1 - b))
    return place


def store_blocks(out, value, first, group, bits):
    height = out.shape[1]
    for b in range(value.shape[0] // height):
        out[slot_of(first + b, group, bits)] = value[b * height : (b + 1) * height, :].astype(BF16)


def mlp_weights_kernel(clips, bits, info, *refs):
    hid, dy, acts, dpre = (refs[n * clips : (n + 1) * clips] for n in range(4))
    down_o, up_o = refs[4 * clips :]
    group = info[1 + clips]
    full = dy[0].shape[0]
    tile = full // 2
    for left, right, out in ((hid, dy, down_o), (acts, dpre, up_o)):
        for m in range(2):
            part = slice(m * tile, (m + 1) * tile)
            acc = dot_nt(left[0][part, :], right[0][...])
            for c in range(1, clips):
                acc = acc + dot_nt(left[c][part, :], right[c][...])
            store_blocks(out, acc, m * tile // out.shape[1], group, bits)


def order_kernel(clips, bits, info, acc, out):
    store_blocks(out, acc[...], 0, info[1 + clips], bits)


def unpack_kernel(clips, bits, info, *refs):
    group = info[1 + clips]
    count = refs[0].shape[0]
    height = refs[0].shape[1]
    sources = refs[: len(refs) // 2]
    for src, dst in zip(sources, refs[len(sources) :]):
        for i in range(count):
            dst[i * height : (i + 1) * height, :] = src[slot_of(i, group, bits)].astype(F32)


def local(
    groups,
    tokens,
    horizon,
    attn_gain,
    attn_shift,
    query_weight,
    key_weight,
    value_weight,
    query_bias,
    value_bias,
    output_weight,
    output_bias,
    mlp_gain,
    mlp_shift,
    up_weight,
    up_bias,
    down_weight,
    down_bias,
    cotangent,
):
    clips, rows, width = tokens.shape
    full = 4 * width
    hidden = up_weight.shape[1]
    padded = -(-rows // QB) * QB
    bits = groups.bit_length() - 1
    t = lax.axis_index("tensor")
    group = lax.axis_index("dp")
    lengths = CONTEXT + FRAME * horizon
    info = jnp.concatenate([t[None], lengths, group[None]]).astype(jnp.int32)

    def core(x):
        return lax.ppermute(x, "tensor", [(i, i ^ 1) for i in range(4)])

    def cross(x):
        return lax.ppermute(x, "tensor", [(i, i ^ 2) for i in range(4)])

    def over_dp(x, b):
        return lax.ppermute(x, "dp", [(i, i ^ (1 << b)) for i in range(groups)])

    def gather(x):
        far = cross(x)
        return (x, core(x), far, core(far))

    def reduce_blocks(x):
        for b in range(bits):
            half = x.shape[0] // 2
            got = over_dp(x[half:], b)
            x = (x[:half].astype(F32) + got.astype(F32)).astype(BF16)
        for b in reversed(range(bits)):
            x = jnp.concatenate([x, over_dp(x, b)], axis=0)
        return x

    def columns(*vectors):
        stacked = jnp.stack(vectors)
        return jnp.broadcast_to(stacked[:, :, None], stacked.shape + (LB,))

    tokens_t = jnp.transpose(tokens, (0, 2, 1))
    cot_t = jnp.transpose(cotangent, (0, 2, 1))
    w_qkv = jnp.concatenate([query_weight.T, key_weight.T, value_weight.T], axis=0)
    b_qkv = columns(jnp.concatenate([query_bias, jnp.zeros_like(query_bias), value_bias]))[0]
    gain1, shift1, gain2, shift2 = columns(attn_gain, attn_shift, mlp_gain, mlp_shift)
    own_gain = columns(
        lax.dynamic_slice_in_dim(attn_gain, t * width, width),
        lax.dynamic_slice_in_dim(mlp_gain, t * width, width),
        down_bias,
    )
    ub = columns(up_bias)[0]

    tok = [gather(tokens_t[c]) for c in range(clips)]
    high = output_bias.astype(BF16)
    low = (output_bias - high.astype(F32)).astype(BF16)
    tail = jnp.pad(jnp.stack([high, low]), ((0, TAIL - 2), (0, full - width)))
    out_w = gather(jnp.concatenate([output_weight, tail], axis=0))
    cot = [gather(cot_t[c]) for c in range(clips)]

    w_back, up_t, down_t = call(
        prep_kernel,
        "prep",
        [struct((full, 3 * width), BF16), struct((hidden, full), BF16), struct((full, hidden), BF16)],
        (info, w_qkv, up_weight, down_weight),
    )
    wo_t, bias_o = call(
        prep_out_kernel,
        "prep_out",
        [struct((full, full), BF16), struct((full, LB), F32)],
        (info,) + out_w,
    )

    pairs = width // HDIM * padded * padded
    wide_bf = struct((full, padded), BF16)
    own_f = struct((width, padded), F32)
    own_bf = struct((width, padded), BF16)
    row8 = struct((8, padded), F32)
    sums8 = struct((8, width), F32)
    p0_s = struct((width + TAIL, padded), F32)
    p2_s = struct((width + TAIL, padded), BF16)

    fwd = []
    for c in range(clips):
        fwd.append(
            call(
                partial(fwd_kernel, c),
                "fwd_%d" % c,
                [wide_bf, wide_bf, struct((3 * width, padded), BF16), own_bf, own_f, row8, row8],
                (info,) + tok[c] + (gain1, shift1, w_qkv, b_qkv),
                flops=6 * padded * full * width + 4 * pairs * 256,
                trans=pairs,
            )
        )

    mlp = []
    for c in range(clips):
        tokc, acts1, qkv, ob, of, lse, stat1 = fwd[c]
        mlp.append(
            call(
                partial(mlp_kernel, c),
                "mlp_%d" % c,
                [wide_bf] * 4
                + [
                    struct((8, hidden), F32),
                    own_f,
                    own_bf,
                    struct((2, 2 * width + TAIL, padded), BF16),
                    p0_s,
                    p2_s,
                    own_f,
                    row8,
                ],
                (info, tokc) + gather(ob) + (wo_t, bias_o, gain2, shift2)
                + (up_weight, up_t, down_weight, down_t, ub, own_gain[2]) + cot[c],
                [pltpu.VMEM((full, padded), F32)] * 2 + [pltpu.VMEM((full, padded), BF16)],
                flops=10 * padded * full * full,
                trans=padded * full,
            )
        )

    part_spec = pl.BlockSpec((1, width + TAIL, padded), lambda n: (0, 0, 0))

    def fold(own, got):
        return (own.astype(F32) + got.astype(F32)).astype(BF16)

    mids = []
    got_all = []
    for c in range(clips):
        r0, r2, s13, p0, p2, normed, stat2 = mlp[c][5:12]
        got = core(s13)
        got_all.append(got)
        far = cross(fold(p2, got[1, : width + TAIL]))
        mids.append(
            call(
                partial(mid_kernel, c),
                "mid_%d" % c,
                [own_f, own_bf, sums8],
                (info, p0, got, far, normed, stat2, cot_t[c], own_gain[1]),
                specs={2: part_spec},
            )
        )

    result = []
    for c in range(clips):
        r0, r2 = mlp[c][5:7]
        far = cross(fold(r2, got_all[c][1, width + TAIL :]))
        total = r0 + got_all[c][0, width + TAIL :].astype(F32) + far.astype(F32)
        result.append(total[:, :rows].astype(BF16))
    result = jnp.transpose(jnp.stack(result), (0, 2, 1))

    height = full // groups
    blocks = struct((groups, height, full), BF16)
    g_down, g_up = call(
        partial(mlp_weights_kernel, clips, bits),
        "mlp_weights",
        [blocks] * 2,
        (info,) + tuple(mlp[c][n] for n in (0, 3, 2, 1) for c in range(clips)),
        flops=4 * clips * padded * full * full,
    )
    g_down = reduce_blocks(g_down)
    g_up = reduce_blocks(g_up)

    bwd = []
    for c in range(clips):
        tokc, acts1, qkv, ob, of, lse, stat1 = fwd[c]
        bwd.append(
            call(
                partial(bwd_kernel, c),
                "bwd_%d" % c,
                [struct((full, full), F32), sums8, p0_s]
                + [struct((2, width + TAIL, padded), BF16), p2_s],
                (info,) + gather(mids[c][1])
                + (output_weight, qkv, of, ob, lse, tokc, acts1, stat1, gain1, w_back)
                + ((bwd[c - 1][0],) if c else ()),
                [
                    pltpu.VMEM((full, padded), BF16),
                    pltpu.VMEM((width, padded), BF16),
                    pltpu.VMEM((3 * width, padded), BF16),
                    pltpu.VMEM((full, padded), F32),
                    pltpu.VMEM((8, padded), F32),
                ],
                flops=16 * padded * full * width + 10 * pairs * 256,
                trans=pairs,
            )
        )

    (g_attn,) = call(
        partial(order_kernel, clips, bits), "order", [blocks], (info, bwd[clips - 1][0])
    )
    g_attn = reduce_blocks(g_attn)

    grads = []
    sums1 = []
    for c in range(clips):
        p0, p13, p2 = bwd[c][2:5]
        got = core(p13)
        far = cross(fold(p2, got[1]))
        out, sums = call(
            final_kernel,
            "final_%d" % c,
            [struct((width, rows), BF16), sums8],
            (info, p0, got, far, tokens_t[c], fwd[c][6], mids[c][0], own_gain[0]),
            specs={2: part_spec},
        )
        grads.append(out)
        sums1.append(sums)
    grads = jnp.transpose(jnp.stack(grads), (0, 2, 1))

    def total_of(values):
        acc = values[0]
        for value in values[1:]:
            acc = acc + value
        return acc

    vec1 = total_of(sums1)
    vec2 = total_of([b[1] for b in bwd])
    vec3 = total_of([m[2] for m in mids])
    vec4 = total_of([m[4] for m in mlp])
    pack = jnp.concatenate([vec1[:2], vec2[:2], vec3[:4], vec4[0].reshape(-1, width)], axis=0)
    for b in range(bits):
        pack = pack + over_dp(pack, b)

    grad_down, grad_up = call(
        partial(unpack_kernel, clips, bits),
        "unpack",
        [struct((full, full), F32)] * 2,
        (info, g_down, g_up),
    )
    (grad_attn,) = call(
        partial(unpack_kernel, clips, bits),
        "unpack_attn",
        [struct((full, full), F32)],
        (info, g_attn),
    )
    grad_q, grad_k, grad_v, grad_out = (
        grad_attn[n * width : (n + 1) * width] for n in range(4)
    )
    return (
        result,
        grads,
        pack[0],
        pack[1],
        grad_q.T,
        grad_k.T,
        grad_v.T,
        pack[2],
        pack[3],
        grad_out,
        pack[4],
        pack[5],
        pack[6],
        grad_up,
        pack[8:].reshape(hidden),
        grad_down,
        pack[7],
    )


def solution(mesh):
    placed = (
        P("dp", None, "tensor"),
        P("dp"),
        P(),
        P(),
        P(None, "tensor"),
        P(None, "tensor"),
        P(None, "tensor"),
        P("tensor"),
        P("tensor"),
        P("tensor", None),
        P("tensor"),
        P(),
        P(),
        P(None, "tensor"),
        P("tensor"),
        P("tensor", None),
        P("tensor"),
        P("dp", None, "tensor"),
    )
    return jax.shard_map(
        partial(local, mesh.shape["dp"]),
        mesh=mesh,
        in_specs=placed,
        out_specs=(
            P("dp", None, "tensor"),
            P("dp", None, "tensor"),
            P("tensor"),
            P("tensor"),
            P(None, "tensor"),
            P(None, "tensor"),
            P(None, "tensor"),
            P("tensor"),
            P("tensor"),
            P("tensor", None),
            P("tensor"),
            P("tensor"),
            P("tensor"),
            P(None, "tensor"),
            P("tensor"),
            P("tensor", None),
            P("tensor"),
        ),
        check_vma=False,
    )
```
